32 devices in a mesh: roll: 8 (over z, core), kvh: 4 (over y, x).
Axes of the slice: x: 2, y: 2, z: 4, core: 2. Of those that a mesh axis runs over, the one named last changes fastest.
Arguments:
- out_grad: bfloat16 [8, 256, 5120], P('roll', 'kvh'), may hold values from -48 to 48
- out_weight: bfloat16 [4, 5, 128, 5120], P('kvh'), may hold values from -0.078125 to 0.078125
- queries: bfloat16 [8, 256, 4, 5, 128], P('roll', None, 'kvh'), may hold values from -16 to 16
- keys_new: bfloat16 [8, 256, 4, 128], P('roll', None, 'kvh'), may hold values from -16 to 16
- values_new: bfloat16 [8, 256, 4, 128], P('roll', None, 'kvh'), may hold values from -6 to 6
- keys_prompt: bfloat16 [2048, 4, 128], P('roll', 'kvh'), may hold values from -6 to 6
- values_prompt: bfloat16 [2048, 4, 128], P('roll', 'kvh'), may hold values from -6 to 6
- offsets: int32 [8], P('roll'), may hold values from 0 to 3840
Outputs:
- grad_queries: bfloat16 [8, 256, 4, 5, 128], P('roll', None, 'kvh')
- grad_keys_new: bfloat16 [8, 256, 4, 128], P('roll', None, 'kvh')
- grad_values_new: bfloat16 [8, 256, 4, 128], P('roll', None, 'kvh')
- grad_keys_prompt: bfloat16 [2048, 4, 128], P('roll', 'kvh')
- grad_values_prompt: bfloat16 [2048, 4, 128], P('roll', 'kvh')
The draws below stay inside these ranges and needn't reach their ends.
Inputs may be any that keep to these rules, and one draw needn't show every extreme that they name: `offsets`: each slice lies inside a response of 4096 tokens.
All inputs are finite; a program needn't handle non-finite values.
Results may differ from the reference program's by a relative error of at most 0.015.
The reference program's roundings to bfloat16 on the way (of `attn_grad`, `query_rot`, `key_rot`, `attn_probs` and `score_grad`) count: a program that leaves them out, or rounds other values in their place, can miss the bound.
Values may be sent and summed in bfloat16 or wider, within the bound.
No kernel may reach another device: no remote copies, remote signals or barrier semaphores. Data moves between devices by JAX's collectives and lax.ppermute only.
A program may use at most 64 MiB of HBM per device.

```python
import jax
import jax.numpy as jnp
from jax import lax

D = 5120
HD = 128
QG = 5
KVH = 4
ROLLOUTS = 8
SEQ = 256
PROMPT = 2048
RESP = 4096


def draw_queries(key, part):
    full_shape = (ROLLOUTS, SEQ, KVH, QG, HD)
    noise_key = jax.random.fold_in(key, 17)
    bulk_values = jnp.clip(2.0 * jax.random.normal(noise_key, full_shape, jnp.float32), -12.0, 12.0)
    return bulk_values.astype(jnp.bfloat16)


def draw_keys_new(key, part):
    full_shape = (ROLLOUTS, SEQ, KVH, HD)
    noise_key = jax.random.fold_in(key, 29)
    bulk_values = jnp.clip(jax.random.normal(noise_key, full_shape, jnp.float32), -6.0, 6.0)
    return bulk_values.astype(jnp.bfloat16)


def with_ends(result, rng, low, top_value):
    extent = result.shape
    index_at = [jax.random.randint(jax.random.fold_in(rng, axis), (), 0, extent[axis]) for axis in range(len(extent))]
    result = result.at[tuple(index_at)].set(low)
    longest = extent.index(max(extent))
    index_at[longest] = (index_at[longest] + 1) % extent[longest]
    return result.at[tuple(index_at)].set(top_value)


def shard_levels(stream_key, dims, cuts, low, high):
    level, own = 1.0, jax.random.fold_in(stream_key, 6)
    for axis_at, blocks in cuts:
        draws = jnp.exp(jax.random.uniform(jax.random.fold_in(own, axis_at), (blocks,), jnp.float32, low / len(cuts), high / len(cuts)))
        level = level * jnp.repeat(draws, dims[axis_at] // blocks).reshape([-1 if axis == axis_at else 1 for axis in range(len(dims))])
    return level


def centred(own_key, extent, spread, reach, cuts=(), held_as=jnp.bfloat16):
    array = spread * jax.random.normal(own_key, extent, jnp.float32)
    if cuts:
        array = array * shard_levels(own_key, extent, cuts, -0.22, 0.18)
    return jnp.clip(array, -reach, reach).astype(held_as)


def setup_inputs(seed: int = 0) -> dict:
    key_list = jax.random.split(jax.random.key(seed), 9)
    out_grad = centred(key_list[0], (ROLLOUTS, SEQ, D), 8.0, 48.0, ((0, 8), (1, 4)))
    out_weight = centred(key_list[1], (KVH, QG, HD, D), D ** -0.5, 0.078125, ((0, 4),))
    queries = draw_queries(jax.random.fold_in(key_list[8], 71), 0)
    keys_new = draw_keys_new(jax.random.fold_in(key_list[8], 71), 0)
    values_new = centred(key_list[4], (ROLLOUTS, SEQ, KVH, HD), 1.0, 6.0, ((0, 8), (2, 4)))
    keys_prompt = centred(key_list[5], (PROMPT, KVH, HD), 1.0, 6.0, ((0, 8), (1, 4)))
    values_prompt = centred(key_list[6], (PROMPT, KVH, HD), 1.0, 6.0, ((0, 8), (1, 4)))
    offsets = with_ends(jax.random.randint(key_list[7], (ROLLOUTS,), 0, RESP - SEQ + 1), jax.random.fold_in(key_list[7], 1), 0, RESP - SEQ).astype(jnp.int32)
    return {"out_grad": out_grad, "out_weight": out_weight, "queries": queries, "keys_new": keys_new, "values_new": values_new, "keys_prompt": keys_prompt, "values_prompt": values_prompt, "offsets": offsets}


theta_base = 1000000.0


def rotation(positions, head_width):
    half_width = head_width // 2
    frequency = jnp.power(theta_base, -(jnp.arange(half_width, dtype=jnp.float32) / half_width))
    angles = positions.astype(jnp.float32)[:, None] * frequency[None, :]
    return jnp.cos(angles), jnp.sin(angles)


def rotate(vectors, cos_part, sin_part, direction):
    half_width = vectors.shape[-1] // 2
    front_half = vectors[..., :half_width]
    back_half = vectors[..., half_width:]
    return jnp.concatenate([front_half * cos_part - direction * back_half * sin_part, back_half * cos_part + direction * front_half * sin_part], axis=-1)


def one_pair(query_head, key_new, value_new, key_prompt, value_prompt, grad_head, cos_part, sin_part):
    seq_len, group_size, head_width = query_head.shape
    prompt_len = key_prompt.shape[0]
    score_scale = head_width ** -0.5
    query_rot = rotate(query_head.astype(jnp.float32), cos_part[:, None, :], sin_part[:, None, :], 1.0).astype(jnp.bfloat16)
    key_rot = rotate(key_new.astype(jnp.float32), cos_part, sin_part, 1.0).astype(jnp.bfloat16)
    all_keys = jnp.concatenate([key_prompt, key_rot], axis=0)
    all_values = jnp.concatenate([value_prompt, value_new], axis=0)
    query_rows = query_rot.reshape(seq_len * group_size, head_width)
    grad_rows = grad_head.reshape(seq_len * group_size, head_width)
    scores = jnp.dot(query_rows, all_keys.T, preferred_element_type=jnp.float32) * score_scale
    column = jnp.arange(prompt_len + seq_len)[None, :]
    row_pos = (jnp.arange(seq_len * group_size) // group_size)[:, None]
    allowed = (column < prompt_len) | (column - prompt_len <= row_pos)
    scores = jnp.where(allowed, scores, -jnp.inf)
    row_max = jnp.max(scores, axis=1, keepdims=True)
    log_total = row_max + jnp.log(jnp.sum(jnp.exp(scores - row_max), axis=1, keepdims=True))
    attn_probs = jnp.exp(scores - log_total).astype(jnp.bfloat16)
    output = jnp.dot(attn_probs, all_values, preferred_element_type=jnp.float32)
    row_delta = jnp.sum(grad_rows.astype(jnp.float32) * output, axis=1, keepdims=True)
    prob_grad = jnp.dot(grad_rows, all_values.T, preferred_element_type=jnp.float32)
    score_grad = (attn_probs.astype(jnp.float32) * (prob_grad - row_delta) * score_scale).astype(jnp.bfloat16)
    query_grad = jnp.dot(score_grad, all_keys, preferred_element_type=jnp.float32).reshape(seq_len, group_size, head_width)
    query_grad = rotate(query_grad, cos_part[:, None, :], sin_part[:, None, :], -1.0).astype(jnp.bfloat16)
    key_grad = jnp.dot(score_grad.T, query_rows, preferred_element_type=jnp.float32)
    value_grad = jnp.dot(attn_probs.T, grad_rows, preferred_element_type=jnp.float32)
    key_new_grad = rotate(key_grad[prompt_len:], cos_part, sin_part, -1.0).astype(jnp.bfloat16)
    return query_grad, key_new_grad, value_grad[prompt_len:].astype(jnp.bfloat16), key_grad[:prompt_len], value_grad[:prompt_len]


def reference(out_grad, out_weight, queries, keys_new, values_new, keys_prompt, values_prompt, offsets):
    attn_grad = jnp.einsum("rsc,ghdc->rsghd", out_grad.astype(jnp.float32), out_weight.astype(jnp.float32)).astype(jnp.bfloat16)

    def roll_step(totals, slices):
        query_roll, key_roll, value_roll, grad_roll, first_pos = slices
        positions = PROMPT + first_pos + jnp.arange(SEQ, dtype=jnp.int32)
        cos_part, sin_part = rotation(positions, HD)

        def head_step(pieces):
            return one_pair(pieces[0], pieces[1], pieces[2], pieces[3], pieces[4], pieces[5], cos_part, sin_part)

        stacked = (jnp.moveaxis(query_roll, 1, 0), jnp.moveaxis(key_roll, 1, 0), jnp.moveaxis(value_roll, 1, 0), jnp.moveaxis(keys_prompt, 1, 0), jnp.moveaxis(values_prompt, 1, 0), jnp.moveaxis(grad_roll, 1, 0))
        query_grad, key_grad, value_grad, prompt_key, prompt_value = lax.map(head_step, stacked)
        totals = (totals[0] + jnp.moveaxis(prompt_key, 0, 1), totals[1] + jnp.moveaxis(prompt_value, 0, 1))
        return totals, (jnp.moveaxis(query_grad, 0, 1), jnp.moveaxis(key_grad, 0, 1), jnp.moveaxis(value_grad, 0, 1))

    zero_sums = jnp.zeros((PROMPT, KVH, HD), jnp.float32)
    sums, grads = lax.scan(roll_step, (zero_sums, zero_sums), (queries, keys_new, values_new, attn_grad, offsets))
    return grads[0], grads[1], grads[2], sums[0].astype(jnp.bfloat16), sums[1].astype(jnp.bfloat16)
```

```python
import functools

import jax
import jax.numpy as jnp
from jax import lax
from jax.experimental import pallas as pl
from jax.experimental.pallas import tpu as pltpu
from jax.sharding import PartitionSpec as P

theta_base = 1000000.0
f32 = jnp.float32
bf16 = jnp.bfloat16


def flip(value, axis_name, mask):
    count = lax.axis_size(axis_name)
    return lax.ppermute(value, axis_name, [(i, i ^ mask) for i in range(count)])


def rope_tables(positions, head_width):
    half_width = head_width // 2
    frequency = jnp.power(theta_base, -(jnp.arange(half_width, dtype=f32) / half_width))
    angles = positions.astype(f32)[:, None] * frequency[None, :]
    cos_part, sin_part = jnp.cos(angles), jnp.sin(angles)
    return (
        jnp.concatenate([cos_part, cos_part], axis=1),
        jnp.concatenate([-sin_part, sin_part], axis=1),
    )


def turn(rows, cos_full, sin_full):
    return rows * cos_full + pltpu.roll(rows, rows.shape[1] // 2, 1) * sin_full


def dot(left, right):
    return jnp.dot(left, right, preferred_element_type=f32)


def fold_rows(block, op):
    return op(block.reshape(block.shape[0] // 8, 8, block.shape[1]), axis=0)


def forward_kernel(scale, chunk_count, *refs):
    q_ref, kn_ref, vn_ref, cos_ref, sin_ref = refs[:5]
    chunk_refs = refs[5 : 5 + chunk_count]
    p_ref, o_ref, qr_ref, kv_ref, s_scr, vt_scr = refs[5 + chunk_count :]
    near = chunk_count
    width = kn_ref.shape[0]

    @pl.when(pl.program_id(0) == 0)
    def _():
        for c in range(chunk_count):
            kv_ref[c] = chunk_refs[c][...]
        kv_ref[near, 0] = turn(kn_ref[...].astype(f32), cos_ref[...], sin_ref[...]).astype(bf16)
        kv_ref[near, 1] = vn_ref[...]
        for c in range(chunk_count + 1):
            vt_scr[c] = kv_ref[c, 1].astype(f32).T.astype(bf16)

    q_rows = turn(q_ref[0].astype(f32), cos_ref[...], sin_ref[...])
    qr_ref[0] = q_rows.astype(bf16)
    q_cols = q_rows.T.astype(bf16)
    top = jnp.full((8, width), -jnp.inf, f32)
    for c in range(chunk_count + 1):
        s = dot(kv_ref[c, 0], q_cols) * scale
        if c == near:
            key_at = lax.broadcasted_iota(jnp.int32, s.shape, 0)
            row_at = lax.broadcasted_iota(jnp.int32, s.shape, 1)
            s = jnp.where(key_at <= row_at, s, -jnp.inf)
        s_scr[c] = s
        top = jnp.maximum(top, fold_rows(s, jnp.max))
    top = jnp.max(top, axis=0, keepdims=True)
    mass = jnp.zeros((8, width), f32)
    for c in range(chunk_count + 1):
        e = jnp.exp(s_scr[c] - top)
        s_scr[c] = e
        mass = mass + fold_rows(e, jnp.sum)
    inverse = 1.0 / jnp.sum(mass, axis=0, keepdims=True)
    out = jnp.zeros(o_ref.shape, f32)
    for c in range(chunk_count + 1):
        p = (s_scr[c] * inverse).astype(bf16)
        p_ref[c] = p
        out = out + dot(vt_scr[c], p)
    o_ref[...] = out


def forward_call(q, k_new, v_new, cos_full, sin_full, chunks, scale):
    heads, seq, width = q.shape
    count = len(chunks)
    chunk_len = chunks[0].shape[1]
    whole = lambda shape: pl.BlockSpec(shape, lambda h: (0,) * len(shape))
    return pl.pallas_call(
        functools.partial(forward_kernel, scale, count),
        grid=(heads,),
        in_specs=[
            pl.BlockSpec((1, seq, width), lambda h: (h, 0, 0)),
            whole((seq, width)),
            whole((seq, width)),
            whole((seq, width)),
            whole((seq, width)),
        ]
        + [whole((2, chunk_len, width))] * count,
        out_specs=[
            pl.BlockSpec((count + 1, chunk_len, seq), lambda h: (0, 0, h)),
            pl.BlockSpec((width, seq), lambda h: (0, h)),
            pl.BlockSpec((1, seq, width), lambda h: (h, 0, 0)),
            whole((count + 1, 2, chunk_len, width)),
        ],
        out_shape=[
            jax.ShapeDtypeStruct((count + 1, chunk_len, heads * seq), bf16),
            jax.ShapeDtypeStruct((width, heads * seq), f32),
            jax.ShapeDtypeStruct((heads, seq, width), bf16),
            jax.ShapeDtypeStruct((count + 1, 2, chunk_len, width), bf16),
        ],
        scratch_shapes=[
            pltpu.VMEM((count + 1, chunk_len, seq), f32),
            pltpu.VMEM((count + 1, width, chunk_len), bf16),
        ],
        cost_estimate=pl.CostEstimate(
            flops=4 * heads * seq * (count + 1) * chunk_len * width,
            bytes_accessed=2 * heads * seq * (count + 1) * chunk_len,
            transcendentals=heads * seq * (count + 1) * chunk_len,
        ),
        name="probabilities",
    )(q, k_new, v_new, cos_full, sin_full, *chunks)


def project_kernel(places, slots_ref, *refs):
    piece_refs = refs[: len(places)]
    w_ref, g_ref, gt_ref, og_scr, acc = refs[len(places) :]
    step = pl.program_id(0)
    for (mask, part, rows, parts), ref in zip(places, piece_refs):
        at = pl.multiple_of(slots_ref[mask] * (rows * parts) + part * rows, rows)
        og_scr[pl.ds(at, rows), :] = ref[...]
    term = lax.dot_general(
        w_ref[...], og_scr[...], (((1,), (1,)), ((), ())), preferred_element_type=f32
    )

    @pl.when(step == 0)
    def _():
        acc[...] = term

    @pl.when(step > 0)
    def _():
        acc[...] += term

    @pl.when(step == pl.num_programs(0) - 1)
    def _():
        heads, seq, width = g_ref.shape
        for h in range(heads):
            cols = acc[h * width : (h + 1) * width, :]
            gt_ref[:, h * seq : (h + 1) * seq] = cols.astype(bf16)
            g_ref[h] = cols.T.astype(bf16)


def project_call(slots, places, pieces, weight, heads):
    outs, depth = weight.shape
    width = outs // heads
    seq = sum(piece.shape[0] for piece in pieces)
    block = max(b for b in range(128, min(depth, 1280) + 1, 128) if depth % b == 0)
    return pl.pallas_call(
        functools.partial(project_kernel, places),
        grid_spec=pltpu.PrefetchScalarGridSpec(
            num_scalar_prefetch=1,
            grid=(depth // block,),
            in_specs=[pl.BlockSpec((p.shape[0], block), lambda k, s: (0, k)) for p in pieces]
            + [pl.BlockSpec((outs, block), lambda k, s: (0, k))],
            out_specs=[
                pl.BlockSpec((heads, seq, width), lambda k, s: (0, 0, 0)),
                pl.BlockSpec((width, heads * seq), lambda k, s: (0, 0)),
            ],
            scratch_shapes=[pltpu.VMEM((seq, block), bf16), pltpu.VMEM((outs, seq), f32)],
        ),
        out_shape=[
            jax.ShapeDtypeStruct((heads, seq, width), bf16),
            jax.ShapeDtypeStruct((width, heads * seq), bf16),
        ],
        cost_estimate=pl.CostEstimate(
            flops=2 * outs * seq * depth,
            bytes_accessed=2 * (outs + seq) * depth,
            transcendentals=0,
        ),
        name="head_cotangent",
    )(slots, *pieces, weight)


def backward_kernel(scale, half, p_ref, kv_ref, q_ref, g_ref, gt_ref, o_ref, cos_ref, sin_ref,
                    odd_ref, even_ref, near_ref, dq_ref, dq_acc, delta):
    step = pl.program_id(0)
    heads, seq, width = q_ref.shape

    @pl.when(step == 0)
    def _():
        delta[...] = jnp.sum(gt_ref[...].astype(f32) * o_ref[...], axis=0, keepdims=True)

    keys = kv_ref[0, 0]
    values = kv_ref[0, 1]
    p = p_ref[0]
    dp = dot(values, gt_ref[...])
    ds = (p.astype(f32) * (dp - delta[...]) * scale).astype(bf16)
    dv = dot(p, g_ref[...].reshape(heads * seq, width))
    dk = dot(ds, q_ref[...].reshape(heads * seq, width))
    dq = dot(keys.astype(f32).T.astype(bf16), ds)

    @pl.when(step == 0)
    def _():
        dq_acc[...] = dq

    @pl.when(step > 0)
    def _():
        dq_acc[...] += dq

    @pl.when(step < half)
    def _():
        odd_ref[0, 0] = dk.astype(bf16)
        odd_ref[0, 1] = dv.astype(bf16)

    @pl.when((step >= half) & (step < 2 * half))
    def _():
        even_ref[0, 0] = dk.astype(bf16)
        even_ref[0, 1] = dv.astype(bf16)

    @pl.when(step == 2 * half)
    def _():
        near_ref[0] = turn(dk, cos_ref[...], -sin_ref[...]).astype(bf16)
        near_ref[1] = dv.astype(bf16)
        for h in range(heads):
            rows = dq_acc[:, h * seq : (h + 1) * seq].T
            dq_ref[h] = turn(rows, cos_ref[...], -sin_ref[...]).astype(bf16)


def backward_call(p, kv, q, g, gt, o, cos_full, sin_full, scale):
    heads, seq, width = q.shape
    count, _, chunk_len, _ = kv.shape
    half = (count - 1) // 2
    whole = lambda shape: pl.BlockSpec(shape, lambda i: (0,) * len(shape))
    block = (1, 2, chunk_len, width)
    return pl.pallas_call(
        functools.partial(backward_kernel, scale, half),
        grid=(count,),
        in_specs=[
            pl.BlockSpec((1, chunk_len, heads * seq), lambda i: (i, 0, 0)),
            pl.BlockSpec(block, lambda i: (i, 0, 0, 0)),
            whole(q.shape),
            whole(g.shape),
            whole(gt.shape),
            whole(o.shape),
            whole(cos_full.shape),
            whole(sin_full.shape),
        ],
        out_specs=[
            pl.BlockSpec(block, lambda i: (jnp.minimum(i, half - 1), 0, 0, 0)),
            pl.BlockSpec(block, lambda i: (jnp.clip(i - half, 0, half - 1), 0, 0, 0)),
            whole((2, chunk_len, width)),
            whole(q.shape),
        ],
        out_shape=[
            jax.ShapeDtypeStruct((half, 2, chunk_len, width), bf16),
            jax.ShapeDtypeStruct((half, 2, chunk_len, width), bf16),
            jax.ShapeDtypeStruct((2, chunk_len, width), bf16),
            jax.ShapeDtypeStruct(q.shape, bf16),
        ],
        scratch_shapes=[
            pltpu.VMEM((width, heads * seq), f32),
            pltpu.VMEM((1, heads * seq), f32),
        ],
        cost_estimate=pl.CostEstimate(
            flops=8 * heads * seq * count * chunk_len * width,
            bytes_accessed=2 * heads * seq * count * chunk_len,
            transcendentals=0,
        ),
        name="gradients",
    )(p, kv, q, g, gt, o, cos_full, sin_full)


def gather_pieces(own, count):
    pieces = {(0, None): own}
    half = own.shape[0] // 2
    for mask in range(1, count):
        if mask & (mask - 1) == 0:
            pieces[mask, None] = flip(own, "kvh", mask)
    halves = lambda mask, part: (
        pieces[mask, None][part * half : (part + 1) * half]
        if (mask, None) in pieces
        else pieces[mask, part]
    )
    for mask in range(1, count):
        low = mask & -mask
        high = 1 << (mask.bit_length() - 1)
        if low != high:
            pieces[mask, 0] = flip(halves(mask ^ low, 0), "kvh", low)
            pieces[mask, 1] = flip(halves(mask ^ high, 1), "kvh", high)
    return pieces


def local(out_grad, out_weight, queries, keys_new, values_new, keys_prompt, values_prompt, offsets):
    _, seq, _, heads, width = queries.shape
    roll_count = lax.axis_size("roll")
    kvh_count = lax.axis_size("kvh")
    prompt_total = keys_prompt.shape[0] * roll_count
    scale = width ** (-0.5)
    chips = roll_count // 2

    pieces = gather_pieces(out_grad[0], kvh_count)
    own = jnp.stack([keys_prompt[:, 0], values_prompt[:, 0]])
    far = list(range(chips - 1, -1, -1))
    even = {m: own if m == 0 else flip(own, "roll", 2 * m) for m in far}
    odd = {m: flip(even[m], "roll", 1) for m in far}
    chunks = [odd[m] for m in far] + [even[m] for m in far]

    positions = prompt_total + offsets[0] + jnp.arange(seq, dtype=jnp.int32)
    cos_full, sin_full = rope_tables(positions, width)
    q = jnp.transpose(queries[0, :, 0], (1, 0, 2))
    p, o, q_rot, kv = forward_call(
        q, keys_new[0, :, 0], values_new[0, :, 0], cos_full, sin_full, chunks, scale
    )

    order = sorted(pieces, key=lambda key: (key[0], key[1] or 0))
    places = tuple(
        (mask, part or 0, pieces[mask, part].shape[0], 1 if part is None else 2)
        for mask, part in order
    )
    slots = lax.axis_index("kvh") ^ jnp.arange(kvh_count, dtype=jnp.int32)
    g, gt = project_call(
        slots, places, [pieces[key] for key in order], out_weight.reshape(heads * width, -1), heads
    )

    odd_sums, even_sums, near, dq = backward_call(p, kv, q_rot, g, gt, o, cos_full, sin_full, scale)
    got = flip(odd_sums, "roll", 1)
    sums = (even_sums.astype(f32) + got.astype(f32)).astype(bf16)
    total = sums[chips - 1].astype(f32)
    for j, m in enumerate(far[:-1]):
        total = total + flip(sums[j], "roll", 2 * m).astype(f32)
    total = total.astype(bf16)
    return (
        jnp.transpose(dq, (1, 0, 2))[None, :, None],
        near[0][None, :, None],
        near[1][None, :, None],
        total[0][:, None],
        total[1][:, None],
    )


def solution(mesh):
    placed = (
        P("roll", "kvh", None),
        P("kvh", None, None, None),
        P("roll", None, "kvh", None, None),
        P("roll", None, "kvh", None),
        P("roll", None, "kvh", None),
        P("roll", "kvh", None),
        P("roll", "kvh", None),
        P("roll"),
    )
    return jax.shard_map(
        local,
        mesh=mesh,
        in_specs=placed,
        out_specs=(
            P("roll", None, "kvh", None, None),
            P("roll", None, "kvh", None),
            P("roll", None, "kvh", None),
            P("roll", "kvh", None),
            P("roll", "kvh", None),
        ),
        check_vma=False,
    )
```

```python
import functools
import math

import jax
import jax.numpy as jnp
from jax import lax
from jax.experimental import pallas as pl
from jax.experimental.pallas import tpu as pltpu
from jax.sharding import PartitionSpec as P


theta_base = 1000000.0
f32 = jnp.float32
bf16 = jnp.bfloat16


def flip(value, axis_name, mask):
    count = lax.axis_size(axis_name)
    return lax.ppermute(value, axis_name, [(i, i ^ mask) for i in range(count)])


def rope_tables(positions, head_width):
    half_width = head_width // 2
    frequency = jnp.power(theta_base, -(jnp.arange(half_width, dtype=f32) / half_width))
    angles = positions.astype(f32)[:, None] * frequency[None, :]
    cos_part, sin_part = jnp.cos(angles), jnp.sin(angles)
    return (
        jnp.concatenate([cos_part, cos_part], axis=1),
        jnp.concatenate([-sin_part, sin_part], axis=1),
    )


def turn(rows, cos_full, sin_full):
    return rows * cos_full + pltpu.roll(rows, rows.shape[1] // 2, 1) * sin_full


def dot(left, right):
    return jnp.dot(left, right, preferred_element_type=f32)


def fold_rows(block, op):
    return op(block.reshape(block.shape[0] // 8, 8, block.shape[1]), axis=0)


def local_call(kernel, out_shape, flops, scratch_shapes=(), in_specs=None, **kwargs):
    return pl.pallas_call(
        kernel,
        out_shape=out_shape,
        in_specs=in_specs,
        out_specs=jax.tree.map(lambda _: vmem, out_shape),
        scratch_shapes=scratch_shapes,
        compiler_params=pltpu.CompilerParams(vmem_limit_bytes=vmem_grant),
        cost_estimate=pl.CostEstimate(flops=flops, bytes_accessed=flops // 512, transcendentals=0),
        **kwargs,
    )


vmem = pl.BlockSpec(memory_space=pltpu.VMEM)
vmem_grant = 24 << 20


def probability_kernel(scale, count, groups, *refs):
    q_ref, kn_ref, vn_ref, cos_ref, sin_ref = refs[:5]
    chunk_refs = refs[5 : 5 + count]
    p_refs = refs[5 + count : 5 + count + len(groups)]
    qr_ref, near_ref, o_ref, s_scr, vt_scr, chunk_scr, sems = refs[5 + count + len(groups) :]
    heads, seq, _ = q_ref.shape
    copies = [
        pltpu.make_async_copy(ref, chunk_scr.at[c], sems.at[c]) for c, ref in enumerate(chunk_refs)
    ]
    for copy in copies:
        copy.start()
    factor = scale * math.log2(math.e)
    near_ref[0] = turn(kn_ref[...].astype(f32), cos_ref[...], sin_ref[...]).astype(bf16)
    near_ref[1] = vn_ref[...]
    chunks = [near_ref] + [chunk_scr.at[c] for c in range(count)]
    goals = {}
    for p_ref, group in zip(p_refs, groups):
        for j, c in enumerate(group):
            goals[c] = p_ref.at[j]
    q_cols = []
    for h in range(heads):
        q_rows = turn(q_ref[h].astype(f32), cos_ref[...], sin_ref[...])
        qr_ref[h] = q_rows.astype(bf16)
        q_cols.append(q_rows.T.astype(bf16))
    tops, masses, outs = {}, {}, {}
    waited = set()
    for t in range(heads + 2):
        for c in range(count + 1):
            if c > 0 and c not in waited:
                copies[c - 1].wait()
                waited.add(c)
            if t == 0:
                vt_scr[c] = chunks[c][1].astype(f32).T.astype(bf16)
            if t < heads:
                s = dot(chunks[c][0], q_cols[t])
                if c == 0:
                    key_at = lax.broadcasted_iota(jnp.int32, s.shape, 0)
                    row_at = lax.broadcasted_iota(jnp.int32, s.shape, 1)
                    s = jnp.where(key_at <= row_at, s, -jnp.inf)
                s_scr[t % 3, c] = s
                top = fold_rows(s, jnp.max)
                tops[t] = jnp.maximum(tops[t], top) if c else top
            if 0 <= t - 1 < heads:
                h = t - 1
                if c == 0:
                    tops[h] = jnp.max(tops[h], axis=0, keepdims=True)
                e = jnp.exp2((s_scr[h % 3, c] - tops[h]) * factor)
                s_scr[h % 3, c] = e
                mass = fold_rows(e, jnp.sum)
                masses[h] = masses[h] + mass if c else mass
            if 0 <= t - 2:
                h = t - 2
                cols = slice(h * seq, (h + 1) * seq)
                if c == 0:
                    masses[h] = 1.0 / jnp.sum(masses[h], axis=0, keepdims=True)
                probs = (s_scr[h % 3, c] * masses[h]).astype(bf16)
                goals[c][:, cols] = probs
                out = dot(vt_scr[c], probs)
                outs[h] = outs[h] + out if c else out
                if c == count:
                    o_ref[:, cols] = outs[h]


def project_kernel(count, slots_ref, *refs):
    w_ref, o_ref = refs[count : count + 2]
    g_ref, gt_ref, delta_ref, og_scr = refs[count + 2 :]
    for i, ref in enumerate(refs[:count]):
        rows = ref.shape[0]
        og_scr[pl.ds(pl.multiple_of(slots_ref[i] * rows, rows), rows), :] = ref[...]
    heads, seq, width = g_ref.shape
    for h in range(heads):
        cols = slice(h * seq, (h + 1) * seq)
        rows = lax.dot_general(
            w_ref[h * width : (h + 1) * width, :],
            og_scr[...],
            (((1,), (1,)), ((), ())),
            preferred_element_type=f32,
        ).astype(bf16)
        gt_ref[:, cols] = rows
        g_ref[h] = rows.astype(f32).T.astype(bf16)
        delta_ref[:, cols] = jnp.sum(rows.astype(f32) * o_ref[:, cols], axis=0, keepdims=True)


def project_call(slots, pieces, weight, o, heads):
    outs, depth = weight.shape
    width = outs // heads
    seq = sum(piece.shape[0] for piece in pieces)
    return local_call(
        functools.partial(project_kernel, len(pieces)),
        [
            jax.ShapeDtypeStruct((heads, seq, width), bf16),
            jax.ShapeDtypeStruct((width, heads * seq), bf16),
            jax.ShapeDtypeStruct((1, heads * seq), f32),
        ],
        2 * outs * seq * depth,
        in_specs=[pl.BlockSpec(memory_space=pltpu.SMEM)] + [vmem] * (len(pieces) + 2),
        scratch_shapes=[pltpu.VMEM((seq, depth), bf16)],
    )(slots, *pieces, weight, o)


def chunk_gradients(scale, p_ref, keys, values, q_ref, g_ref, gt_ref, delta_ref, add_dq):
    heads, seq, _ = q_ref.shape
    keys_t = keys.astype(f32).T.astype(bf16)
    dk = dv = None
    for h in range(heads):
        cols = slice(h * seq, (h + 1) * seq)
        p = p_ref[:, cols]
        dp = dot(values, gt_ref[:, cols])
        ds = (p.astype(f32) * (dp - delta_ref[:, cols]) * scale).astype(bf16)
        dv_h = dot(p, g_ref[h])
        dk_h = dot(ds, q_ref[h])
        dk, dv = (dk_h, dv_h) if dk is None else (dk + dk_h, dv + dv_h)
        add_dq(cols, dot(keys_t, ds))
    return dk, dv


def gradient_kernel(scale, count, got_at, is_last, split, *refs):
    it = iter(refs)
    take = lambda n: [next(it) for _ in range(n)]
    p_ref, q_ref, g_ref, gt_ref, delta_ref = take(5)
    chunk_refs = take(count)
    got_ref = next(it) if got_at is not None else None
    if is_last:
        near_ref, cos_ref, sin_ref, *dq_refs = take(7)
    out_refs = take(count if split else 1)
    if is_last:
        near_out, dq_out = take(2)
    dq_acc = next(it)
    started = []

    def add_dq(cols, term):
        if cols.start in started:
            dq_acc[:, cols] += term
        else:
            started.append(cols.start)
            dq_acc[:, cols] = term

    first = 1 if is_last else 0
    common = (q_ref, g_ref, gt_ref, delta_ref, add_dq)
    if is_last:
        dk, dv = chunk_gradients(scale, p_ref.at[0], near_ref[0], near_ref[1], *common)
        near_out[0] = turn(dk, cos_ref[...], -sin_ref[...]).astype(bf16)
        near_out[1] = dv.astype(bf16)
    for j, chunk in enumerate(chunk_refs):
        dk, dv = chunk_gradients(scale, p_ref.at[first + j], chunk[0], chunk[1], *common)
        if got_at is not None:
            dk = dk + got_ref[got_at + j, 0].astype(f32)
            dv = dv + got_ref[got_at + j, 1].astype(f32)
        to = out_refs[j] if split else out_refs[0].at[j]
        to[0] = dk.astype(to.dtype)
        to[1] = dv.astype(to.dtype)
    if is_last:
        heads, seq, _ = q_ref.shape
        for h in range(heads):
            cols = slice(h * seq, (h + 1) * seq)
            total = dq_acc[:, cols]
            for ref in dq_refs:
                total = total + ref[:, cols]
            dq_out[h] = turn(total.T, cos_ref[...], -sin_ref[...]).astype(bf16)


def gradient_call(scale, p, common, chunks, got=None, got_at=None, last=None, kinds=None):
    q = common[0]
    heads, seq, width = q.shape
    count = len(chunks)
    shape = chunks[0].shape
    if kinds is None:
        out_shape = [jax.ShapeDtypeStruct((count, *shape), bf16)]
    else:
        out_shape = [jax.ShapeDtypeStruct(shape, kind) for kind in kinds]
    operands = [p, *common, *chunks] + ([got] if got is not None else []) + list(last or ())
    dq_shape = (width, heads * seq)
    scratch = []
    if last:
        out_shape += [jax.ShapeDtypeStruct(shape, bf16), jax.ShapeDtypeStruct(q.shape, bf16)]
        scratch = [pltpu.VMEM(dq_shape, f32)]
    else:
        out_shape += [jax.ShapeDtypeStruct(dq_shape, f32)]
    return local_call(
        functools.partial(
            gradient_kernel, scale, count, got_at, bool(last), kinds is not None
        ),
        out_shape,
        8 * heads * seq * p.shape[0] * p.shape[1] * width,
        in_specs=[vmem] * len(operands),
        scratch_shapes=scratch,
    )(*operands)


def gather_pieces(own):
    rolls, count = lax.axis_size("roll"), lax.axis_size("kvh")
    bits = count.bit_length() - 1
    if count != 1 << bits:
        raise ValueError("unsupported mesh")
    turned = lambda mask, core: sum(
        1 << ((k + core) % bits) for k in range(bits) if mask & (1 << k)
    )
    pieces = [own]
    for mask in range(1, count):
        high = 1 << (mask.bit_length() - 1)
        pairs = [
            (r * count + k, r * count + (k ^ turned(high, r % 2)))
            for r in range(rolls)
            for k in range(count)
        ]
        pieces.append(lax.ppermute(pieces[mask ^ high], ("roll", "kvh"), pairs))
    core = lax.axis_index("roll") % 2
    masks = [jnp.array([turned(m, c) for m in range(count)], jnp.int32) for c in range(2)]
    return pieces, lax.axis_index("kvh") ^ jnp.where(core == 0, *masks)


def body(out_grad, out_weight, queries, keys_new, values_new, keys_prompt, values_prompt, offsets):
    _, seq, _, heads, width = queries.shape
    roll_count = lax.axis_size("roll")
    chunk_len = keys_prompt.shape[0]
    prompt_total = chunk_len * roll_count
    scale = width ** (-0.5)
    chips = roll_count // 2
    if chips < 2 or chunk_len != seq:
        raise ValueError("unsupported mesh")
    far = list(range(chips - 1, 1, -1))
    shape = jax.ShapeDtypeStruct
    rows = heads * seq

    pieces, slots = gather_pieces(out_grad[0])
    even = {0: jnp.stack([keys_prompt[:, 0], values_prompt[:, 0]])}
    for m in far + [1]:
        even[m] = flip(even[0], "roll", 2 * m)
    odd = {}
    for m in [0, 1] + far:
        odd[m] = flip(even[m], "roll", 1)

    positions = prompt_total + offsets[0] + jnp.arange(seq, dtype=jnp.int32)
    cos_full, sin_full = rope_tables(positions, width)
    q = jnp.transpose(queries[0, :, 0], (1, 0, 2))
    chunks = [even[0], odd[0], even[1], odd[1]] + [even[m] for m in far] + [odd[m] for m in far]
    n = len(far)
    groups = (range(5 + n, 5 + 2 * n), range(5, 5 + n), (4, 2), (3,), (0, 1))
    *probs, q_rot, near, o = local_call(
        functools.partial(probability_kernel, scale, len(chunks), groups),
        [shape((len(group), seq, rows), bf16) for group in groups]
        + [shape(q.shape, bf16), shape((2, seq, width), bf16), shape((width, rows), f32)],
        4 * rows * (1 + len(chunks)) * seq * width,
        in_specs=[vmem] * 5 + [pl.BlockSpec(memory_space=pl.ANY)] * len(chunks),
        scratch_shapes=[
            pltpu.VMEM((3, len(chunks) + 1, seq, seq), f32),
            pltpu.VMEM((len(chunks) + 1, width, seq), bf16),
            pltpu.VMEM((len(chunks), 2, seq, width), bf16),
            pltpu.SemaphoreType.DMA((len(chunks),)),
        ],
    )(q, keys_new[0, :, 0], values_new[0, :, 0], cos_full, sin_full, *chunks)
    p_odd, p_even, p_close, p_one, p_near = probs

    g, gt, delta = project_call(
        slots, pieces, out_weight.reshape(heads * width, -1), o, heads
    )

    common = (q_rot, g, gt, delta)
    sums, dq1 = gradient_call(scale, p_odd, common, [odd[m] for m in far])
    got = flip(sums, "roll", 1)
    *sums, dq2 = gradient_call(
        scale, p_even, common, [even[m] for m in far], got, 0, kinds=[bf16] * len(far)
    )
    arrived = []
    for m, part in zip(far, sums):
        arrived.append(flip(part, "roll", 2 * m))
    sums, dq3 = gradient_call(scale, p_close, common, [odd[1], odd[0]])
    got = flip(sums, "roll", 1)
    part, dq4 = gradient_call(scale, p_one, common, [even[1]], got, 0, kinds=[bf16])
    arrived.append(flip(part, "roll", 2))
    total, near_grads, dq = gradient_call(
        scale, p_near, common, [even[0]], got, 1,
        last=(near, cos_full, sin_full, dq1, dq2, dq3, dq4), kinds=[f32],
    )
    for part in arrived:
        total = total + part.astype(f32)
    total = total.astype(bf16)
    return (
        jnp.transpose(dq, (1, 0, 2))[None, :, None],
        near_grads[0][None, :, None],
        near_grads[1][None, :, None],
        total[0][:, None],
        total[1][:, None],
    )


def solution(mesh):
    placed = (
        P("roll", "kvh", None),
        P("kvh", None, None, None),
        P("roll", None, "kvh", None, None),
        P("roll", None, "kvh", None),
        P("roll", None, "kvh", None),
        P("roll", "kvh", None),
        P("roll", "kvh", None),
        P("roll"),
    )
    return jax.shard_map(
        body,
        mesh=mesh,
        in_specs=placed,
        out_specs=(
            P("roll", None, "kvh", None, None),
            P("roll", None, "kvh", None),
            P("roll", None, "kvh", None),
            P("roll", "kvh", None),
            P("roll", "kvh", None),
        ),
        check_vma=False,
    )
```
